32 devices in a mesh: groups: 2 (over y), tile: 16 (over z, x, core).
Axes of the slice: x: 2, y: 2, z: 4, core: 2. Of those that a mesh axis runs over, the one named last changes fastest.
Arguments:
- features: bfloat16 [1024, 24, 2048], P(('groups', 'tile')), parts along dimension 0, may hold values from 0 to 64, as said below
- aerial_image: bfloat16 [3, 8192, 192], P(None, ('groups', 'tile')), parts along dimension 1, may hold values from -4 to 4
- blocks: int32 [64, 2], P('groups'), parts along dimension 0, may hold values from 0 to 127, as said below
- routes: int32 [64, 1], P('groups'), parts along dimension 0, may hold values from 0 to 15; in each aligned block of 32 rows (0 to 31, 32 to 63, ...) at most 4 rows name the same one
- w_one: bfloat16 [2048, 256], replicated, may hold values from -0.125 to 0.125
- w_depth: bfloat16 [3, 9, 2048], replicated, may hold values from -2 to 2
- w_rates: bfloat16 [3, 2048, 256], replicated, may hold values from -0.125 to 0.125
- w_pool: bfloat16 [2048, 256], replicated, may hold values from -0.125 to 0.125
- w_proj: bfloat16 [1280, 256], replicated, may hold values from -0.15625 to 0.15625
- w_first: bfloat16 [16, 9, 256, 256], P('tile'), may hold values from -0.125 to 0.125
- w_color: bfloat16 [16, 27, 256], P('tile'), may hold values from -1.25 to 1.25
- w_second: bfloat16 [16, 9, 256, 256], P('tile'), may hold values from -0.125 to 0.125
- w_head: bfloat16 [16, 6, 256], P('tile'), may hold values from -0.375 to 0.375
Outputs:
- aspp_features: bfloat16 [1024, 24, 256], P(('groups', 'tile')), parts along dimension 0
- context: float32 [512], P('groups'), parts along dimension 0
- refined: bfloat16 [64, 6, 1024], P(('groups', 'tile')), parts along dimension 0
The draws below stay inside these ranges and needn't reach their ends.
There are 2 independent parts, one for each index of `groups`. The reference program is written for one: setup_inputs(seed, part) draws one part's arguments, and reference() takes and returns one part's arrays. A program takes and returns all parts, laid end to end along the dimension named above; an argument that names none is the same for every part. Nothing has to cross between parts.
Inputs may be any that keep to these rules, and one draw needn't show every extreme that they name: `features`: Non-negative activations. Blocks are distinct; block rows lie below 128 and block columns below 6; no strip of 32 feature rows holds more than 6 blocks and one holds exactly 6. `routes`: at most 4 blocks go to one refiner and one refiner receives exactly 4; every refiner receives one or more.
All inputs are finite; a program needn't handle non-finite values.
Results may differ from the reference program's by a relative error of at most 0.0065.
Values may be sent and summed in bfloat16 or wider, within the bound.
A program may use at most 128 MiB of HBM per device.

```python
import math
import jax
import jax.numpy as jnp
import numpy as np
from jax import lax

C_IN = 2048
A = 256
REF = 256
NCLS = 6
R_DEV = 32
COLS = 24
BLK = 32
CAP = 4
OWN = 6
NB = 32
NROWS = 512
EXPERTS = 16
STRIP_BLOCK_ROWS = 8
REGION_BLOCK_COLUMNS = 6
GRID = 48


def draw_features(key, part):
    key_base, key_rows, key_cols, key_chan = jax.random.split(jax.random.fold_in(key, 11), 4)
    rows_at = jnp.arange(NROWS, dtype=jnp.float32) / max(NROWS - 1, 1)
    row_jitter = jnp.exp(jax.random.uniform(key_rows, (NROWS,), minval=-0.5, maxval=0.5))
    col_scale = jnp.exp(jax.random.uniform(key_cols, (COLS,), minval=-0.5, maxval=0.5))
    chan_scale = jnp.exp(jax.random.uniform(key_chan, (C_IN,), minval=-0.7, maxval=0.7))
    base = jnp.minimum(jnp.abs(jax.random.normal(key_base, (NROWS, COLS, C_IN))), 5.0)
    rising = 3.0 ** rows_at
    values = 0.6 * base * (rising * row_jitter)[:, None, None] * col_scale[None, :, None] * chan_scale[None, None, :]
    return values.astype(jnp.float32).astype(jnp.bfloat16)


def draw_blocks(key, part):
    key_order, key_full, key_place, key_shuffle = jax.random.split(jax.random.fold_in(key, 23), 4)
    strip_count = NROWS // R_DEV
    slot_total = strip_count * OWN
    order_perm = jax.random.permutation(key_order, slot_total)
    slot_rank = jnp.argsort(order_perm)
    full_strip = jax.random.randint(key_full, (), 0, strip_count)
    slot_ids = jnp.arange(slot_total, dtype=jnp.int32)
    score = jnp.where(slot_ids // OWN == full_strip, slot_ids - slot_total, slot_rank.astype(jnp.int32))
    chosen = jnp.argsort(score)[:NB].astype(jnp.int32)
    chosen = chosen[jax.random.permutation(key_shuffle, NB)]
    strip_index_list = chosen // OWN
    within = chosen % OWN
    spacing = GRID // OWN
    block_location = within * spacing + jax.random.randint(key_place, (NB,), 0, spacing)
    block_row_count = strip_index_list * STRIP_BLOCK_ROWS + block_location // REGION_BLOCK_COLUMNS
    block_cols = block_location % REGION_BLOCK_COLUMNS
    return jnp.stack([block_row_count, block_cols], axis=1).astype(jnp.int32)


def level_of(rng, dims, shards, smallest, high):
    def one(dim, shards_of):
        heights = jax.random.uniform(jax.random.fold_in(jax.random.fold_in(rng, 6), dim), (shards_of,), jnp.float32, smallest / len(shards), high / len(shards))
        return jnp.repeat(jnp.exp(heights), dims[dim] // shards_of).reshape((-1,) + (1,) * (len(dims) - dim - 1))

    loudness = one(*shards[0])
    for cut in shards[1:]:
        loudness = loudness * one(*cut)
    return loudness


def routed_block(own_key, own, number, rows, count, top, reach, lean):
    sequence = jax.random.permutation(own_key, count)
    heavy_load, common = load_shares(count, rows * top, reach, lean, True), load_shares(count, rows * top, reach, lean, False)
    places = jnp.arange(count)

    def named(lengths, rotation):
        used = int((lengths > 0).sum())
        fixed = max(1, used // 4)
        passed = fixed + (places - fixed + rotation * (used - fixed)) % max(1, count - fixed)
        return jnp.zeros((count,), jnp.int32).at[sequence[jnp.where(places < fixed, places, passed)]].set(jnp.asarray(lengths, jnp.int32))

    lengths = jnp.where(number % 4 == 0, named(heavy_load, number // 4), named(common, number - number // 4 - 1))
    mixed = jax.random.permutation(jax.random.fold_in(own, 3), count)
    giver, taker = mixed[0:count // 2 * 2:2], mixed[1:count // 2 * 2:2]
    room = jnp.minimum(lengths[giver] - 1, reach - lengths[taker]) // 2
    room = jnp.where((giver == sequence[0]) | (taker == sequence[0]) | (lengths[taker] == 0), 0, jnp.maximum(room, 0))
    passed = jax.random.randint(jax.random.fold_in(own, 4), (count // 2,), 0, 1 << 20) % (room + 1)
    lengths = lengths.at[giver].add(-passed).at[taker].add(passed)
    items = jnp.searchsorted(jnp.cumsum(lengths), jnp.arange(rows * top), side="right").astype(jnp.int32)
    listing = items.reshape(top, rows).T
    listing = listing[jax.random.permutation(jax.random.fold_in(own, 1), rows)]
    rotation = jax.random.randint(jax.random.fold_in(own, 2), (rows, 1), 0, top)
    return jnp.take_along_axis(listing, (jnp.arange(top)[None, :] + rotation) % top, axis=1)


def load_shares(count, total, reach, slope, full):
    loads = [(1 << 20) // math.isqrt(grade ** slope) + 1 for grade in range(1, count + 1)]
    largest = reach if full else min(reach, max(-(-total // count), total * loads[0] // sum(loads)))
    least = 1 if total - largest >= count - 1 else 0
    counts, rest = [largest] + [least] * (count - 1), total - largest - least * (count - 1)
    while rest > 0:
        candidates = [i for i in range(1, count) if counts[i] < largest] or [i for i in range(1, count) if counts[i] < reach]
        whole, budget = sum([loads[i] for i in candidates]), rest
        for i in candidates:
            more = min(reach - counts[i], max(1, budget * loads[i] // whole), rest)
            counts[i] = counts[i] + more
            rest = rest - more
    return np.array(counts)


def bell_draw(rng, extent, width, most, cuts=(), kind=jnp.bfloat16):
    factor_of = level_of(rng, extent, cuts, -0.22, 0.18) if cuts else 1.0
    array = jax.random.normal(rng, extent, jnp.float32) * width * factor_of
    return jnp.minimum(jnp.maximum(array, -most), most).astype(kind)


def setup_inputs(seed: int = 0, part: int = 0) -> dict:
    seeds = jax.random.split(jax.random.key(seed), 14)
    part_keys = jax.random.split(jax.random.fold_in(seeds[13], part), 14)
    features = draw_features(jax.random.fold_in(jax.random.fold_in(seeds[13], part), 71), part)
    aerial_image = bell_draw(part_keys[1], (3, NROWS * 8, COLS * 8), 1.0, 4.0, ((1, 16),))
    blocks = draw_blocks(jax.random.fold_in(jax.random.fold_in(seeds[13], part), 71), part)
    routes_keys = jax.random.split(jax.random.fold_in(part_keys[3], 1), NB // NB)
    routes_turns = jax.random.permutation(jax.random.fold_in(part_keys[3], 3), NB // NB)
    routes = jax.vmap(lambda own, number: routed_block(jax.random.fold_in(part_keys[3], 2), own, number, NB, EXPERTS, 1, CAP, 2))(routes_keys, routes_turns).reshape((NB, 1))
    w_one = bell_draw(seeds[4], (C_IN, A), C_IN ** -0.5, 0.125)
    w_depth = bell_draw(seeds[5], (3, 9, C_IN), 9 ** -0.5, 2.0)
    w_rates = bell_draw(seeds[6], (3, C_IN, A), C_IN ** -0.5, 0.125)
    w_pool = bell_draw(seeds[7], (C_IN, A), C_IN ** -0.5, 0.125)
    w_proj = bell_draw(seeds[8], (5 * A, A), (5 * A) ** -0.5, 0.15625)
    w_first = bell_draw(seeds[9], (EXPERTS, 9, A, REF), (9 * A) ** -0.5, 0.125, ((0, 16),))
    w_color = bell_draw(seeds[10], (EXPERTS, 27, REF), 27 ** -0.5, 1.25, ((0, 16),))
    w_second = bell_draw(seeds[11], (EXPERTS, 9, REF, REF), (9 * REF) ** -0.5, 0.125, ((0, 16),))
    w_head = bell_draw(seeds[12], (EXPERTS, NCLS, REF), REF ** -0.5, 0.375, ((0, 16),))
    return dict(features=features, aerial_image=aerial_image, blocks=blocks, routes=routes, w_one=w_one, w_depth=w_depth, w_rates=w_rates, w_pool=w_pool, w_proj=w_proj, w_first=w_first, w_color=w_color, w_second=w_second, w_head=w_head)


atrous_rates = (6, 12, 18)
reach_rows = 18


def upsample_table(block_side):
    cells = block_side // 8
    pixels = jnp.arange(block_side, dtype=jnp.float32)
    source = jnp.clip((pixels + 0.5) / 8.0 - 0.5, 0.0, float(cells - 1))
    centres = jnp.arange(cells, dtype=jnp.float32)
    weights_table = jnp.maximum(1.0 - jnp.abs(source[:, None] - centres[None, :]), 0.0)
    return (weights_table[:, None, :, None] * weights_table[None, :, None, :]).reshape(block_side * block_side, cells * cells)


def conv_taps(inputs, kernel):
    block_count, block_side = inputs.shape[0], inputs.shape[1]
    padded = jnp.pad(inputs, ((0, 0), (1, 1), (1, 1), (0, 0)))
    running = jnp.zeros((block_count * block_side * block_side, kernel.shape[2]), jnp.float32)
    for kernel_tap in range(9):
        row_off, col_off = kernel_tap // 3, kernel_tap % 3
        window = padded[:, row_off:row_off + block_side, col_off:col_off + block_side, :]
        running = running + jnp.dot(window.reshape(block_count * block_side * block_side, -1), kernel[kernel_tap], preferred_element_type=jnp.float32)
    return running


def conv_color(colors, kernel):
    block_count, block_side = colors.shape[0], colors.shape[2]
    padded = jnp.pad(colors, ((0, 0), (0, 0), (1, 1), (1, 1)))
    running = jnp.zeros((block_count, block_side, block_side, kernel.shape[1]), jnp.float32)
    for kernel_tap in range(9):
        row_off, col_off = kernel_tap // 3, kernel_tap % 3
        window = padded[:, :, row_off:row_off + block_side, col_off:col_off + block_side]
        running = running + jnp.einsum("scpq,cr->spqr", window.astype(jnp.float32), kernel[3 * kernel_tap:3 * kernel_tap + 3].astype(jnp.float32))
    return running.reshape(block_count * block_side * block_side, -1)


def refine(crop_data, colors, w_first, w_color, w_second, w_head):
    block_count, block_side = colors.shape[0], colors.shape[2]
    upsampled = jnp.einsum("pk,ska->spa", upsample_table(block_side), crop_data.astype(jnp.float32), precision=lax.Precision.HIGHEST)
    upsampled = upsampled.astype(jnp.bfloat16).reshape(block_count, block_side, block_side, -1)
    first_maps = conv_taps(upsampled, w_first) + conv_color(colors, w_color)
    first_maps = jnp.maximum(first_maps, 0.0).astype(jnp.bfloat16).reshape(block_count, block_side, block_side, -1)
    second = jnp.maximum(conv_taps(first_maps, w_second), 0.0).astype(jnp.bfloat16)
    second = second.reshape(block_count, block_side * block_side, -1)
    logits = jnp.einsum("spr,nr->snp", second.astype(jnp.float32), w_head.astype(jnp.float32))
    return logits.astype(jnp.bfloat16)


def reference(features, aerial_image, blocks, routes, w_one, w_depth, w_rates, w_pool, w_proj, w_first, w_color, w_second, w_head):
    height, col_count, channels = features.shape
    branch_width = w_one.shape[1]
    cells = BLK // 8
    running = jnp.sum(features, axis=(0, 1), dtype=jnp.float32)
    pooled = running / (height * col_count)
    context = jnp.maximum(jnp.dot(pooled, w_pool.astype(jnp.float32), precision=lax.Precision.HIGHEST), 0.0)
    offset_amount = jnp.dot(context, w_proj[4 * branch_width:].astype(jnp.float32), precision=lax.Precision.HIGHEST)
    padded = jnp.pad(features, ((reach_rows, reach_rows), (reach_rows, reach_rows), (0, 0)))
    depth_weights = w_depth.astype(jnp.float32)

    def strip_output(strip_id):
        window = lax.dynamic_slice_in_dim(padded, (strip_id * R_DEV).astype(jnp.int32), R_DEV + 2 * reach_rows, 0)
        centre_cells = window[reach_rows:reach_rows + R_DEV, reach_rows:reach_rows + col_count, :].reshape(R_DEV * col_count, channels)
        branches = [jnp.maximum(jnp.dot(centre_cells, w_one, preferred_element_type=jnp.float32), 0.0)]
        for branch_id, dilation in enumerate(atrous_rates):
            running_sum = jnp.zeros((R_DEV, col_count, channels), jnp.float32)
            for kernel_tap in range(9):
                row_at = reach_rows + (kernel_tap // 3 - 1) * dilation
                col_at = reach_rows + (kernel_tap % 3 - 1) * dilation
                running_sum = running_sum + window[row_at:row_at + R_DEV, col_at:col_at + col_count, :] * depth_weights[branch_id, kernel_tap]
            depth_map = jnp.maximum(running_sum, 0.0).astype(jnp.bfloat16)
            branches.append(jnp.maximum(jnp.dot(depth_map.reshape(R_DEV * col_count, channels), w_rates[branch_id], preferred_element_type=jnp.float32), 0.0))
        stacked = jnp.concatenate(branches, axis=1).astype(jnp.bfloat16)
        blended_sum = jnp.dot(stacked, w_proj[:4 * branch_width], preferred_element_type=jnp.float32) + offset_amount
        return jnp.maximum(blended_sum, 0.0).astype(jnp.bfloat16).reshape(R_DEV, col_count, branch_width)

    aspp_features = lax.map(strip_output, jnp.arange(height // R_DEV, dtype=jnp.int32)).reshape(height, col_count, branch_width)

    def one_block(block_id):
        row_at = blocks[block_id, 0].astype(jnp.int32)
        col_at = blocks[block_id, 1].astype(jnp.int32)
        expert_id = routes[block_id, 0].astype(jnp.int32)
        zero_index = jnp.zeros((), jnp.int32)
        crop_data = lax.dynamic_slice(aspp_features, (cells * row_at, cells * col_at, zero_index), (cells, cells, branch_width)).reshape(1, cells * cells, branch_width)
        colors = lax.dynamic_slice(aerial_image, (zero_index, row_at * BLK, col_at * BLK), (3, BLK, BLK))[None]
        return refine(crop_data, colors, w_first[expert_id], w_color[expert_id], w_second[expert_id], w_head[expert_id])[0]

    refined = lax.map(one_block, jnp.arange(NB, dtype=jnp.int32))
    return (aspp_features, context, refined)
```

```python
import functools

import jax
import jax.numpy as jnp
import numpy as np
from jax import lax
from jax.experimental import pallas as pl
from jax.experimental.pallas import tpu as pltpu
from jax.sharding import PartitionSpec as P

BLK = 32
CAP = 4
CELLS = 4
RATES = (6, 12, 18)
REACH = 18
CHUNK = 256
F32 = jnp.float32
BF16 = jnp.bfloat16


def split_three(value):
    high = value.astype(BF16)
    rest = value - high.astype(F32)
    mid = rest.astype(BF16)
    low = (rest - mid.astype(F32)).astype(BF16)
    return high, mid, low


def exact_row_dot(row, weights):
    high, mid, low = split_three(row)
    stacked = jnp.concatenate(
        [high.astype(F32), mid.astype(F32), low.astype(F32), jnp.zeros((13, row.shape[1]), F32)], axis=0
    ).astype(BF16)
    product = jnp.dot(stacked, weights, preferred_element_type=F32)
    return product[0:1] + product[1:2] + product[2:3]


def pyramid_kernel(
    tiles, rows, cols, channels, width,
    feat_hbm, w_one_hbm, w_rates_hbm, w_depth_ref, w_pool_hbm, w_proj_hbm, slots_ref, colors_hbm,
    aspp_ref, context_ref, crops_ref, mine_ref,
    feat, w_one, w_rates, w_pool, w_proj, halo, grown, depth, acc, sums, sums_in, crops_out, crops_in, colors_in,
    local_sem, halo_send, halo_recv, sum_send, sum_recv, color_send, color_recv, crop_send, crop_recv,
):
    me = lax.axis_index("tile")
    chunks = channels // CHUNK
    edge = REACH * cols
    cells = rows * cols

    local = [
        pltpu.make_async_copy(source, target, local_sem.at[n])
        for n, (source, target) in enumerate(
            ((feat_hbm, feat), (w_one_hbm, w_one), (w_rates_hbm, w_rates), (w_pool_hbm, w_pool), (w_proj_hbm, w_proj),
             (colors_hbm.at[me], colors_in.at[me]))
        )
    ]
    for copy in local:
        copy.start()

    barrier = pltpu.get_barrier_semaphore()

    def greet(step, carry):
        peer = lax.rem(me + step, tiles)
        pl.semaphore_signal(barrier, inc=1, device_id={"tile": peer}, device_id_type=pl.DeviceIdType.MESH)
        return carry

    lax.fori_loop(1, tiles, greet, 0)
    pl.semaphore_wait(barrier, tiles - 1)

    def halo_copy(side, c):
        lanes = pl.ds(pl.multiple_of(c * CHUNK, CHUNK), CHUNK)
        first = cells - edge if side == 0 else 0
        return pltpu.make_async_remote_copy(
            src_ref=feat_hbm.at[pl.ds(first, edge), lanes],
            dst_ref=halo.at[side, :, lanes],
            send_sem=halo_send.at[side, c],
            recv_sem=halo_recv.at[side, c],
            device_id={"tile": lax.rem(me + 1, tiles) if side == 0 else lax.rem(me + tiles - 1, tiles)},
            device_id_type=pl.DeviceIdType.MESH,
        )

    has_next = me < tiles - 1
    has_prev = me > 0

    def send_halo(c, carry):
        @pl.when(has_next)
        def _():
            halo_copy(0, c).start()

        @pl.when(has_prev)
        def _():
            halo_copy(1, c).start()

        return carry

    lax.fori_loop(0, chunks, send_halo, 0)

    def peer_copy(step, source, target, send, recv):
        return pltpu.make_async_remote_copy(
            src_ref=source, dst_ref=target, send_sem=send.at[step], recv_sem=recv.at[step],
            device_id={"tile": lax.rem(me + step, tiles)}, device_id_type=pl.DeviceIdType.MESH,
        )

    def sum_copy(step):
        return peer_copy(step, sums, sums_in.at[step], sum_send, sum_recv)

    def color_copy(step):
        peer = lax.rem(me + step, tiles)
        return peer_copy(step, colors_hbm.at[peer], colors_in.at[me], color_send, color_recv)

    def crop_copy(step):
        peer = lax.rem(me + step, tiles)
        return peer_copy(step, crops_out.at[peer], crops_in.at[me], crop_send, crop_recv)

    def each_peer(function):
        def body(step, carry):
            function(step)
            return carry

        lax.fori_loop(1, tiles, body, 0)

    local[0].wait()

    def sum_rows(n, totals):
        block = feat[pl.ds(pl.multiple_of(n * 16, 16), 16), :].astype(F32)
        return totals + block[0:8] + block[8:16]

    totals = lax.fori_loop(0, cells // 16, sum_rows, jnp.zeros((8, channels), F32))
    sums[...] = jnp.sum(totals, axis=0, keepdims=True)
    each_peer(lambda step: sum_copy(step).start())
    each_peer(lambda step: color_copy(step).start())

    local[1].wait()
    local[2].wait()
    tall = 256

    @pl.loop(0, cells // tall)
    def _(m):
        span = pl.ds(pl.multiple_of(m * tall, tall), tall)
        acc[0, span, :] = jnp.dot(feat[span, :], w_one[...], preferred_element_type=F32)
        for k in range(3):
            acc[k + 1, span, :] = jnp.zeros((tall, width), F32)

    @pl.when(jnp.logical_not(has_prev))
    def _():
        grown[0:edge, :] = jnp.zeros((edge, CHUNK), F32)

    @pl.when(jnp.logical_not(has_next))
    def _():
        grown[edge + cells :, :] = jnp.zeros((edge, CHUNK), F32)

    def widen(source, start, count, lanes):
        @pl.loop(0, count // 48)
        def _(n):
            grown[pl.ds(pl.multiple_of(start + n * 48, 8), 48), :] = source[
                pl.ds(pl.multiple_of(n * 48, 16), 48), lanes
            ].astype(F32)

    def one_chunk(c, carry):
        lanes = pl.ds(pl.multiple_of(c * CHUNK, CHUNK), CHUNK)
        widen(feat, edge, cells, lanes)

        @pl.when(has_prev)
        def _():
            halo_copy(0, c).wait_recv()
            widen(halo.at[0], 0, edge, lanes)

        @pl.when(has_next)
        def _():
            halo_copy(1, c).wait_recv()
            widen(halo.at[1], edge + cells, edge, lanes)

        for half in range(CHUNK // 128):
            inner = slice(half * 128, half * 128 + 128)
            outer = pl.ds(pl.multiple_of(c * CHUNK + half * 128, 128), 128)
            for k, d in enumerate(RATES):
                taps = [
                    jnp.broadcast_to(w_depth_ref[9 * k + t : 9 * k + t + 1, outer].astype(F32), (8, 128)) for t in range(9)
                ]

                def weigh(parts, column, taps=taps):
                    total = None
                    for i in range(3):
                        tap = jnp.concatenate([taps[3 * i + column]] * (parts[i].shape[0] // 8), axis=0)
                        term = parts[i] * tap
                        total = term if total is None else total + term
                    return total

                @pl.loop(0, rows // 2, unroll=2)
                def _(pair, d=d, weigh=weigh, inner=inner, k=k):
                    results = []
                    for r in range(2):
                        parts = []
                        for i in (-1, 0, 1):
                            start = pl.multiple_of((REACH + i * d + r) * cols + pair * (2 * cols), 8)
                            parts.append(grown[pl.ds(start, cols), inner])
                        low = -(-(cols - d) // 8) * 8
                        high = (d // 8) * 8
                        middle = weigh(parts, 1)
                        left = weigh([p[:low] for p in parts], 0)
                        right = weigh([p[high:] for p in parts], 2)
                        fill = jnp.zeros((d, 128), F32)
                        left = jnp.concatenate([fill, left[: cols - d]], axis=0)
                        right = jnp.concatenate([right[d - high :], fill], axis=0)
                        results.append(jnp.maximum(middle + left + right, 0.0))
                    depth[k, pl.ds(pl.multiple_of(pair * (2 * cols), 16), 2 * cols), inner] = jnp.concatenate(
                        results, axis=0
                    ).astype(BF16)

        for k in range(3):
            @pl.loop(0, cells // tall)
            def _(m, k=k):
                span = pl.ds(pl.multiple_of(m * tall, tall), tall)
                acc[k + 1, span, :] += jnp.dot(depth[k, span, :], w_rates[k, lanes, :], preferred_element_type=F32)

        return carry

    lax.fori_loop(0, chunks, one_chunk, 0)

    each_peer(lambda step: sum_copy(step).wait_recv())

    def add_sums(step, total):
        return total + sums_in[step]

    total = lax.fori_loop(1, tiles, add_sums, sums[...])
    pooled = total / (cells * tiles)
    local[3].wait()
    local[4].wait()
    context = jnp.maximum(exact_row_dot(pooled, w_pool[...]), 0.0)
    context_ref[...] = context
    offset = exact_row_dot(context, w_proj[4 * width :, :])

    @pl.loop(0, cells // tall)
    def _(m):
        span = pl.ds(pl.multiple_of(m * tall, tall), tall)
        blended = jnp.broadcast_to(offset, (tall, width))
        for k in range(4):
            branch = jnp.maximum(acc[k, span, :], 0.0).astype(BF16)
            blended += jnp.dot(branch, w_proj[k * width : (k + 1) * width, :], preferred_element_type=F32)
        aspp_ref[span, :] = jnp.maximum(blended, 0.0).astype(BF16)

    per = CAP * CELLS * CELLS

    def cut(n, carry):
        wanted = slots_ref[pl.ds(pl.multiple_of(n * per, per), per), 0:1]
        chosen = (lax.broadcasted_iota(jnp.int32, (per, cells), 1) == wanted).astype(F32).astype(BF16)
        crops_out[n] = jnp.dot(chosen, aspp_ref[...], preferred_element_type=F32).astype(BF16)
        return carry

    lax.fori_loop(0, tiles, cut, 0)
    crops_in[me] = crops_out[me]
    each_peer(lambda step: crop_copy(step).start())
    local[5].wait()
    each_peer(lambda step: color_copy(step).wait_recv())

    def add_colors(n, total):
        return total + colors_in[n].astype(F32)

    mine_ref[...] = lax.fori_loop(0, tiles, add_colors, jnp.zeros(mine_ref.shape, F32))
    each_peer(lambda step: crop_copy(step).wait_recv())

    def add_crops(n, total):
        return total + crops_in[n].astype(F32)

    crops_ref[...] = lax.fori_loop(0, tiles, add_crops, jnp.zeros(crops_ref.shape, F32)).astype(BF16)

    def drain(step):
        sum_copy(step).wait_send()
        color_copy(step).wait_send()
        crop_copy(step).wait_send()

    each_peer(drain)

    def drain_halo(c, carry):
        @pl.when(has_next)
        def _():
            halo_copy(0, c).wait_send()

        @pl.when(has_prev)
        def _():
            halo_copy(1, c).wait_send()

        return carry

    lax.fori_loop(0, chunks, drain_halo, 0)


def pyramid(tiles, rows, cols, features, w_one, w_rates, w_depth, w_pool, w_proj, slots, colors):
    channels, width = w_one.shape
    cells = rows * cols
    per = CAP * CELLS * CELLS
    chunks = channels // CHUNK
    edge = REACH * cols
    whole = pl.BlockSpec(memory_space=pltpu.VMEM)
    away = pl.BlockSpec(memory_space=pl.ANY)
    dma = pltpu.SemaphoreType.DMA
    return pl.pallas_call(
        functools.partial(pyramid_kernel, tiles, rows, cols, channels, width),
        out_shape=(
            jax.ShapeDtypeStruct((cells, width), BF16),
            jax.ShapeDtypeStruct((1, width), F32),
            jax.ShapeDtypeStruct((per, width), BF16),
            jax.ShapeDtypeStruct((16, 1024), F32),
        ),
        in_specs=[away, away, away, whole, away, away, whole, away],
        out_specs=(whole, whole, whole, whole),
        scratch_shapes=[
            pltpu.VMEM((cells, channels), BF16),
            pltpu.VMEM(w_one.shape, BF16),
            pltpu.VMEM(w_rates.shape, BF16),
            pltpu.VMEM(w_pool.shape, BF16),
            pltpu.VMEM(w_proj.shape, BF16),
            pltpu.VMEM((2, edge, channels), BF16),
            pltpu.VMEM((cells + 2 * edge, CHUNK), F32),
            pltpu.VMEM((3, cells, CHUNK), BF16),
            pltpu.VMEM((4, cells, width), F32),
            pltpu.VMEM((1, channels), F32),
            pltpu.VMEM((tiles, 1, channels), F32),
            pltpu.VMEM((tiles, per, width), BF16),
            pltpu.VMEM((tiles, per, width), BF16),
            pltpu.VMEM((tiles, 16, 1024), BF16),
            dma((6,)),
            dma((2, chunks)),
            dma((2, chunks)),
            dma((tiles,)),
            dma((tiles,)),
            dma((tiles,)),
            dma((tiles,)),
            dma((tiles,)),
            dma((tiles,)),
        ],
        compiler_params=pltpu.CompilerParams(collective_id=0, has_side_effects=True, vmem_limit_bytes=52 << 20),
        name="pyramid",
    )(features.reshape(cells, channels), w_one, w_rates, w_depth.reshape(27, channels), w_pool, w_proj, slots, colors)


def refine_kernel(crops_ref, mine_ref, table_ref, first_ref, color_ref, second_ref, head_ref, out_ref, grid_a, grid_b, patches):
    side, pixels = BLK, BLK * BLK
    width = first_ref.shape[1]
    lane = lax.broadcasted_iota(jnp.int32, (16, pixels), 1)
    row_at, col_at = lane // side, lane % side
    colors = mine_ref[...]
    pieces = []
    for i in (-1, 0, 1):
        for j in (-1, 0, 1):
            moved = colors if i == 0 and j == 0 else pltpu.roll(colors, (-(side * i + j)) % pixels, 1)
            inside = (row_at + i >= 0) & (row_at + i < side) & (col_at + j >= 0) & (col_at + j < side)
            pieces.append(jnp.where(inside, moved, 0.0))
    patches[...] = jnp.concatenate(pieces, axis=0).T.astype(BF16)
    blank = jnp.zeros((side, 3 * width), BF16)
    for grid_ref in (grid_a, grid_b):
        grid_ref[0:side, :] = blank
        grid_ref[side + pixels :, :] = blank
    tall = 256
    col = lax.broadcasted_iota(jnp.int32, (tall, width), 0) % side

    @pl.loop(0, CAP)
    def _(block):
        crop = crops_ref[pl.ds(pl.multiple_of(block * 16, 16), 16), :]

        @pl.loop(0, pixels // tall)
        def _(m):
            at = pl.multiple_of(m * tall, tall)
            for j in range(3):
                up = jnp.dot(table_ref[j, pl.ds(at, tall), :], crop, preferred_element_type=F32)
                grid_a[pl.ds(pl.multiple_of(side + at, side), tall), j * width : (j + 1) * width] = up.astype(BF16)

        @pl.loop(0, pixels // tall)
        def _(m):
            at = pl.multiple_of(m * tall, tall)
            total = jnp.dot(patches[pl.ds(at, tall), :], color_ref[block], preferred_element_type=F32)
            for i in range(3):
                total += jnp.dot(
                    grid_a[pl.ds(pl.multiple_of(at + side * i, side), tall), :],
                    first_ref[3 * width * i : 3 * width * (i + 1), :],
                    preferred_element_type=F32,
                )
            total = jnp.maximum(total, 0.0)
            before = jnp.where(col == 0, 0.0, pltpu.roll(total, 1, 0))
            after = jnp.where(col == side - 1, 0.0, pltpu.roll(total, tall - 1, 0))
            inner = pl.ds(pl.multiple_of(side + at, side), tall)
            grid_b[inner, 0:width] = before.astype(BF16)
            grid_b[inner, width : 2 * width] = total.astype(BF16)
            grid_b[inner, 2 * width :] = after.astype(BF16)

        @pl.loop(0, pixels // tall)
        def _(m):
            at = pl.multiple_of(m * tall, tall)
            total = jnp.zeros((tall, width), F32)
            for i in range(3):
                total += jnp.dot(
                    grid_b[pl.ds(pl.multiple_of(at + side * i, side), tall), :],
                    second_ref[3 * width * i : 3 * width * (i + 1), :],
                    preferred_element_type=F32,
                )
            total = jnp.maximum(total, 0.0).astype(BF16)
            scores = lax.dot_general(
                head_ref[...], total, (((1,), (1,)), ((), ())), preferred_element_type=F32
            )
            out_ref[block, :, pl.ds(at, tall)] = scores.astype(BF16)


def upsample_tables():
    pixels = np.arange(BLK, dtype=np.float32)
    source = np.clip((pixels + 0.5) / 8.0 - 0.5, 0.0, CELLS - 1.0)
    table = np.maximum(1.0 - np.abs(source[:, None] - np.arange(CELLS, dtype=np.float32)[None, :]), 0.0)
    tables = []
    for j in (-1, 0, 1):
        moved = np.zeros_like(table)
        for q in range(BLK):
            if 0 <= q + j < BLK:
                moved[q] = table[q + j]
        tables.append((table[:, None, :, None] * moved[None, :, None, :]).reshape(BLK * BLK, CELLS * CELLS))
    return np.stack(tables)


def refine(crops, mine, w_first, w_color, w_second, w_head):
    width = w_first.shape[1]
    classes = w_head.shape[0]
    placed = jnp.zeros((CAP, 9, CAP, 4, width), BF16)
    taps = w_color.reshape(9, 3, width)
    for slot in range(CAP):
        placed = placed.at[slot, :, slot, :3, :].set(taps)
    head = jnp.pad(w_head, ((0, 16 - classes), (0, 0)))
    whole = pl.BlockSpec(memory_space=pltpu.VMEM)
    pixels = BLK * BLK
    scores = pl.pallas_call(
        refine_kernel,
        out_shape=jax.ShapeDtypeStruct((CAP, 16, pixels), BF16),
        in_specs=[whole] * 7,
        out_specs=whole,
        scratch_shapes=[
            pltpu.VMEM((pixels + 2 * BLK, 3 * width), BF16),
            pltpu.VMEM((pixels + 2 * BLK, 3 * width), BF16),
            pltpu.VMEM((pixels, 144), BF16),
        ],
        compiler_params=pltpu.CompilerParams(vmem_limit_bytes=40 << 20),
        name="refine",
    )(
        crops,
        mine,
        jnp.asarray(upsample_tables(), BF16),
        w_first.reshape(9 * width, width),
        placed.reshape(CAP, 144, width),
        w_second.reshape(9 * width, width),
        head,
    )
    return scores[:, :classes, :]


def shards(
    tiles,
    features,
    aerial_image,
    blocks,
    routes,
    w_one,
    w_depth,
    w_rates,
    w_pool,
    w_proj,
    w_first,
    w_color,
    w_second,
    w_head,
):
    rows, cols, channels = features.shape
    width = w_one.shape[1]
    me = lax.axis_index("tile")
    count = blocks.shape[0]
    per_holder = count // tiles
    strip_blocks = rows * 8 // BLK
    across = cols // CELLS
    block_row, block_col, experts = blocks[:, 0], blocks[:, 1], routes[:, 0]
    owners = block_row // strip_blocks
    positions = jnp.arange(count, dtype=jnp.int32)
    earlier = positions[None, :] < positions[:, None]
    rank = jnp.sum(earlier & (experts[:, None] == experts[None, :]), axis=1)
    slot_of = experts * CAP + rank
    local_row = block_row - owners * strip_blocks
    place = local_row * across + block_col
    mine_here = owners == me
    slot_hit = (slot_of[None, :] == jnp.arange(tiles * CAP, dtype=jnp.int32)[:, None]) & mine_here[None, :]
    slot_place = jnp.max(jnp.where(slot_hit, place[None, :], -1), axis=1)
    pieces = aerial_image.reshape(3, strip_blocks, BLK, across, BLK).transpose(1, 3, 0, 2, 4)
    pieces = pieces.reshape(strip_blocks * across, 3 * BLK * BLK)
    chosen = (slot_place[:, None] == jnp.arange(strip_blocks * across, dtype=jnp.int32)[None, :]).astype(BF16)
    colors = jnp.dot(chosen, pieces, preferred_element_type=F32).astype(BF16).reshape(tiles, CAP, 3, BLK * BLK)
    colors = jnp.pad(colors, ((0, 0), (0, 0), (0, 1), (0, 0))).reshape(tiles, CAP * 4, BLK * BLK)
    cell = jnp.arange(CELLS * CELLS, dtype=jnp.int32)
    top = slot_place // across * CELLS
    left = slot_place % across * CELLS
    cell_at = (top[:, None] + cell[None, :] // CELLS) * cols + left[:, None] + cell[None, :] % CELLS
    cell_at = jnp.where(slot_place[:, None] >= 0, cell_at, -1).reshape(tiles * CAP * CELLS * CELLS, 1)
    aspp, context, crops, mine = pyramid(
        tiles, rows, cols, features, w_one, w_rates, w_depth, w_pool, w_proj, cell_at, colors
    )
    result = refine(crops, mine, w_first[0], w_color[0], w_second[0], w_head[0])
    pick = ((experts == me)[:, None] & (rank[:, None] == jnp.arange(CAP)[None, :])).astype(BF16)
    send_back = jnp.dot(pick, result.reshape(CAP, -1), preferred_element_type=F32).astype(BF16)
    arrived = lax.all_to_all(
        send_back.reshape(tiles, per_holder, result.shape[1], result.shape[2]), "tile", split_axis=0, concat_axis=0, tiled=True
    )
    refined = jnp.sum(arrived, axis=0, dtype=F32).astype(BF16)
    return aspp.reshape(rows, cols, width), context.reshape(width), refined


def solution(mesh):
    return jax.shard_map(
        functools.partial(shards, mesh.shape["tile"]),
        mesh=mesh,
        in_specs=(
            P(("groups", "tile"), None, None),
            P(None, ("groups", "tile"), None),
            P("groups", None),
            P("groups", None),
            P(),
            P(),
            P(),
            P(),
            P(),
            P("tile", None, None, None),
            P("tile", None, None),
            P("tile", None, None, None),
            P("tile", None, None),
        ),
        out_specs=(
            P(("groups", "tile"), None, None),
            P("groups"),
            P(("groups", "tile"), None, None),
        ),
        check_vma=False,
    )
```

```python
import functools

import jax
import jax.numpy as jnp
import numpy as np
from jax import lax
from jax.experimental import pallas as pl
from jax.experimental.pallas import tpu as pltpu
from jax.sharding import PartitionSpec as P

BLK = 32
CAP = 4
CELLS = 4
RATES = (6, 12, 18)
REACH = 18
CHUNK = 256
F32 = jnp.float32
BF16 = jnp.bfloat16


def split_three(value):
    high = value.astype(BF16)
    rest = value - high.astype(F32)
    mid = rest.astype(BF16)
    low = (rest - mid.astype(F32)).astype(BF16)
    return high, mid, low


def exact_row_dot(row, weights):
    high, mid, low = split_three(row)
    stacked = jnp.concatenate(
        [high.astype(F32), mid.astype(F32), low.astype(F32), jnp.zeros((13, row.shape[1]), F32)], axis=0
    ).astype(BF16)
    product = jnp.dot(stacked, weights, preferred_element_type=F32)
    return product[0:1] + product[1:2] + product[2:3]


def pyramid_kernel(
    tiles, rows, cols, channels, width,
    feat_hbm, w_one_hbm, w_rates_hbm, w_depth_ref, w_pool_hbm, w_proj_hbm, image_hbm, first_hbm, second_hbm,
    color_ref, head_ref, table_ref, blocks_ref, routes_ref,
    aspp_ref, context_ref, refined_ref,
    image, first, second, crops_ref, mine_ref, grid_a, grid_b, patches, scores, back_out, back_in, colors_out, back_send, back_recv,
    feat, w_one, w_rates, w_pool, w_proj, halo, grown, depth, acc, sums, sums_in, crops_out, crops_in, colors_in,
    local_sem, halo_send, halo_recv, sum_send, sum_recv, color_send, color_recv, crop_send, crop_recv,
):
    me = lax.axis_index("tile")
    chunks = channels // CHUNK
    edge = REACH * cols
    cells = rows * cols
    count = routes_ref.shape[1]
    held = count // tiles * 8

    local = [
        pltpu.make_async_copy(source, target, local_sem.at[n])
        for n, (source, target) in enumerate(
            ((feat_hbm, feat), (w_one_hbm, w_one), (w_rates_hbm, w_rates), (w_pool_hbm, w_pool), (w_proj_hbm, w_proj),
             (image_hbm, image), (first_hbm, first), (second_hbm, second))
        )
    ]
    for copy in local:
        copy.start()

    barrier = pltpu.get_barrier_semaphore()

    def greet(step, carry):
        peer = lax.rem(me + step, tiles)
        pl.semaphore_signal(barrier, inc=1, device_id={"tile": peer}, device_id_type=pl.DeviceIdType.MESH)
        return carry

    lax.fori_loop(1, tiles, greet, 0)
    pl.semaphore_wait(barrier, tiles - 1)

    def halo_copy(side, c):
        lanes = pl.ds(pl.multiple_of(c * CHUNK, CHUNK), CHUNK)
        first = cells - edge if side == 0 else 0
        return pltpu.make_async_remote_copy(
            src_ref=feat_hbm.at[pl.ds(first, edge), lanes],
            dst_ref=halo.at[side, :, lanes],
            send_sem=halo_send.at[side, c],
            recv_sem=halo_recv.at[side, c],
            device_id={"tile": lax.rem(me + 1, tiles) if side == 0 else lax.rem(me + tiles - 1, tiles)},
            device_id_type=pl.DeviceIdType.MESH,
        )

    has_next = me < tiles - 1
    has_prev = me > 0

    def send_halo(c, carry):
        @pl.when(has_next)
        def _():
            halo_copy(0, c).start()

        @pl.when(has_prev)
        def _():
            halo_copy(1, c).start()

        return carry

    lax.fori_loop(0, chunks, send_halo, 0)

    def peer_copy(step, source, target, send, recv):
        return pltpu.make_async_remote_copy(
            src_ref=source, dst_ref=target, send_sem=send.at[step], recv_sem=recv.at[step],
            device_id={"tile": lax.rem(me + step, tiles)}, device_id_type=pl.DeviceIdType.MESH,
        )

    def sum_copy(step):
        return peer_copy(step, sums, sums_in.at[step], sum_send, sum_recv)

    def color_copy(step):
        peer = lax.rem(me + step, tiles)
        return peer_copy(step, colors_out.at[pl.ds(pl.multiple_of(peer * 16, 16), 16)], colors_in.at[me], color_send, color_recv)

    def crop_copy(step):
        peer = lax.rem(me + step, tiles)
        return peer_copy(step, crops_out.at[peer], crops_in.at[me], crop_send, crop_recv)

    def back_copy(step):
        peer = lax.rem(me + step, tiles)
        return peer_copy(
            step, back_out.at[pl.ds(pl.multiple_of(peer * held, held), held)], back_in.at[me], back_send, back_recv
        )

    def each_peer(function):
        def body(step, carry):
            function(step)
            return carry

        lax.fori_loop(1, tiles, body, 0)

    local[0].wait()

    def sum_rows(n, totals):
        block = feat[pl.ds(pl.multiple_of(n * 16, 16), 16), :].astype(F32)
        return totals + block[0:8] + block[8:16]

    totals = lax.fori_loop(0, cells // 16, sum_rows, jnp.zeros((8, channels), F32))
    sums[...] = jnp.sum(totals, axis=0, keepdims=True)
    each_peer(lambda step: sum_copy(step).start())

    local[1].wait()
    local[2].wait()
    tall = 256

    @pl.loop(0, cells // tall)
    def _(m):
        span = pl.ds(pl.multiple_of(m * tall, tall), tall)
        acc[0, span, :] = jnp.dot(feat[span, :], w_one[...], preferred_element_type=F32)
        for k in range(3):
            acc[k + 1, span, :] = jnp.zeros((tall, width), F32)

    @pl.when(jnp.logical_not(has_prev))
    def _():
        grown[0:edge, :] = jnp.zeros((edge, CHUNK), F32)

    @pl.when(jnp.logical_not(has_next))
    def _():
        grown[edge + cells :, :] = jnp.zeros((edge, CHUNK), F32)

    def widen(source, start, count, lanes):
        @pl.loop(0, count // 48)
        def _(n):
            grown[pl.ds(pl.multiple_of(start + n * 48, 8), 48), :] = source[
                pl.ds(pl.multiple_of(n * 48, 16), 48), lanes
            ].astype(F32)

    experts = routes_ref[...].astype(F32)
    square = (count, count)
    down, over = lax.broadcasted_iota(jnp.int32, square, 0), lax.broadcasted_iota(jnp.int32, square, 1)
    spread = jnp.broadcast_to(experts, square)
    upright = jnp.sum(jnp.where(down == over, spread, 0.0), axis=1, keepdims=True)
    rank = jnp.sum(jnp.where((upright == spread) & (down < over), 1.0, 0.0), axis=0, keepdims=True)
    slot_of = experts * CAP + rank
    strip_blocks = rows // CELLS
    local_row = blocks_ref[0:1, :].astype(F32) - lax.convert_element_type(me * strip_blocks, F32)
    is_mine = (local_row >= 0) & (local_row < strip_blocks)
    base = jnp.where(is_mine, local_row * (CELLS * cols) + blocks_ref[1:2, :].astype(F32) * CELLS, -1e6)
    to_me = jnp.where(experts == lax.convert_element_type(me, F32), rank, -1.0)

    def lookup(slot, values, fill):
        shape = (slot.shape[0], count)
        hit = jnp.broadcast_to(slot, shape) == jnp.broadcast_to(slot_of, shape)
        return jnp.max(jnp.where(hit, jnp.broadcast_to(values, shape), fill), axis=1, keepdims=True)

    local[5].wait()
    parts_high = image.shape[0]
    across = parts_high // 3
    group = 256
    line = lax.broadcasted_iota(jnp.int32, (group, 1), 0)
    lane = lax.broadcasted_iota(jnp.int32, (1, BLK * BLK), 1)
    source = lax.broadcasted_iota(jnp.int32, (1, parts_high), 1)
    source_channel = (source >= across).astype(jnp.int32) + (source >= 2 * across).astype(jnp.int32)
    source_block = (source - source_channel * across) // BLK
    deep = lax.broadcasted_iota(jnp.int32, (parts_high, 1), 0)
    keep = ((deep & (BLK - 1)) == (lane & (BLK - 1)))
    tall_rows = image.shape[1]
    image_row = lax.broadcasted_iota(jnp.int32, (tall_rows, 1), 0)
    colors_out[...] = jnp.zeros(colors_out.shape, BF16)

    @pl.loop(0, strip_blocks)
    def _(at):
        select = (image_row == at * BLK + (lane >> 5)).astype(F32).astype(BF16)
        strips = jnp.dot(image[...], select, preferred_element_type=F32)
        strips = jnp.where(keep, strips, 0.0).astype(BF16)

        @pl.loop(0, tiles * 16 // group)
        def _(n):
            row = line + n * group
            found = lookup((row >> 2).astype(F32), base, -1e6)
            wanted = (at * (CELLS * cols) + source_block * CELLS).astype(F32)
            chosen = ((found == wanted) & ((row & 3) == source_channel)).astype(F32).astype(BF16)
            span = pl.ds(pl.multiple_of(n * group, group), group)
            colors_out[span, :] += jnp.dot(chosen, strips, preferred_element_type=F32).astype(BF16)

    def one_chunk(c, carry):
        @pl.when(c == chunks - 2)
        def _():
            each_peer(lambda step: color_copy(step).start())

        lanes = pl.ds(pl.multiple_of(c * CHUNK, CHUNK), CHUNK)
        widen(feat, edge, cells, lanes)

        @pl.when(has_prev)
        def _():
            halo_copy(0, c).wait_recv()
            widen(halo.at[0], 0, edge, lanes)

        @pl.when(has_next)
        def _():
            halo_copy(1, c).wait_recv()
            widen(halo.at[1], edge + cells, edge, lanes)

        for half in range(CHUNK // 128):
            inner = slice(half * 128, half * 128 + 128)
            outer = pl.ds(pl.multiple_of(c * CHUNK + half * 128, 128), 128)
            for k, d in enumerate(RATES):
                taps = [
                    jnp.broadcast_to(w_depth_ref[t, k : k + 1, outer].astype(F32), (8, 128)) for t in range(9)
                ]

                def weigh(parts, column, taps=taps):
                    total = None
                    for i in range(3):
                        tap = jnp.concatenate([taps[3 * i + column]] * (parts[i].shape[0] // 8), axis=0)
                        term = parts[i] * tap
                        total = term if total is None else total + term
                    return total

                @pl.loop(0, rows // 2, unroll=2)
                def _(pair, d=d, weigh=weigh, inner=inner, k=k):
                    results = []
                    for r in range(2):
                        parts = []
                        for i in (-1, 0, 1):
                            start = pl.multiple_of((REACH + i * d + r) * cols + pair * (2 * cols), 8)
                            parts.append(grown[pl.ds(start, cols), inner])
                        low = -(-(cols - d) // 8) * 8
                        high = (d // 8) * 8
                        middle = weigh(parts, 1)
                        left = weigh([p[:low] for p in parts], 0)
                        right = weigh([p[high:] for p in parts], 2)
                        fill = jnp.zeros((d, 128), F32)
                        left = jnp.concatenate([fill, left[: cols - d]], axis=0)
                        right = jnp.concatenate([right[d - high :], fill], axis=0)
                        results.append(jnp.maximum(middle + left + right, 0.0))
                    depth[k, pl.ds(pl.multiple_of(pair * (2 * cols), 16), 2 * cols), inner] = jnp.concatenate(
                        results, axis=0
                    ).astype(BF16)

        for k in range(3):
            @pl.loop(0, cells // tall)
            def _(m, k=k):
                span = pl.ds(pl.multiple_of(m * tall, tall), tall)
                acc[k + 1, span, :] += jnp.dot(depth[k, span, :], w_rates[k, lanes, :], preferred_element_type=F32)

        return carry

    lax.fori_loop(0, chunks, one_chunk, 0)

    each_peer(lambda step: sum_copy(step).wait_recv())

    def add_sums(step, total):
        return total + sums_in[step]

    total = lax.fori_loop(1, tiles, add_sums, sums[...])
    pooled = total / (cells * tiles)
    local[3].wait()
    local[4].wait()
    context = jnp.maximum(exact_row_dot(pooled, w_pool[...]), 0.0)
    context_ref[...] = context
    offset = exact_row_dot(context, w_proj[4 * width :, :])

    @pl.loop(0, cells // tall)
    def _(m):
        span = pl.ds(pl.multiple_of(m * tall, tall), tall)
        blended = jnp.broadcast_to(offset, (tall, width))
        for k in range(4):
            branch = jnp.maximum(acc[k, span, :], 0.0).astype(BF16)
            blended += jnp.dot(branch, w_proj[k * width : (k + 1) * width, :], preferred_element_type=F32)
        aspp_ref[span, :] = jnp.maximum(blended, 0.0).astype(BF16)

    per = CAP * CELLS * CELLS
    cell_row = lax.broadcasted_iota(jnp.int32, (per, 1), 0)

    def cut(n, carry):
        slot = (n * CAP + (cell_row >> 4)).astype(F32)
        wanted = lookup(slot, base, -1e6) + (((cell_row >> 2) & 3) * cols + (cell_row & 3)).astype(F32)
        chosen = (lax.broadcasted_iota(jnp.int32, (per, cells), 1).astype(F32) == wanted).astype(F32).astype(BF16)
        crops_out[n] = jnp.dot(chosen, aspp_ref[...], preferred_element_type=F32).astype(BF16)
        return carry

    lax.fori_loop(0, tiles, cut, 0)
    crops_in[me] = crops_out[me]
    each_peer(lambda step: crop_copy(step).start())
    colors_in[me] = colors_out[pl.ds(pl.multiple_of(me * 16, 16), 16), :]
    each_peer(lambda step: color_copy(step).wait_recv())

    def add_colors(n, total):
        return total + colors_in[n].astype(F32)

    mine_ref[...] = lax.fori_loop(0, tiles, add_colors, jnp.zeros(mine_ref.shape, F32))
    side, pixels = BLK, BLK * BLK
    wide = lax.broadcasted_iota(jnp.int32, (16, pixels), 1)
    row_at, col_at = wide >> 5, wide & (side - 1)
    colors = mine_ref[...]
    pieces = []
    for i in (-1, 0, 1):
        for j in (-1, 0, 1):
            moved = colors if i == 0 and j == 0 else pltpu.roll(colors, (-(side * i + j)) % pixels, 1)
            inside = (row_at + i >= 0) & (row_at + i < side) & (col_at + j >= 0) & (col_at + j < side)
            pieces.append(jnp.where(inside, moved, 0.0))
    patches[...] = jnp.concatenate(pieces, axis=0).T.astype(BF16)
    blank = jnp.zeros((side, 3 * width), BF16)
    for grid_ref in (grid_a, grid_b):
        grid_ref[0:side, :] = blank
        grid_ref[side + pixels :, :] = blank
    tall = 512
    local[6].wait()
    local[7].wait()
    scores[...] = jnp.zeros(scores.shape, F32)
    col = lax.broadcasted_iota(jnp.int32, (tall, width), 0) & (side - 1)

    each_peer(lambda step: crop_copy(step).wait_recv())

    def add_crops(n, total):
        return total + crops_in[n].astype(F32)

    crops_ref[...] = lax.fori_loop(0, tiles, add_crops, jnp.zeros(crops_ref.shape, F32)).astype(BF16)

    @pl.loop(0, CAP)
    def _(block):
        tap_row = lax.broadcasted_iota(jnp.int32, (144, 27), 0)
        channel = (tap_row & 15) - block * 4
        wanted_tap = (tap_row >> 4) * 3 + channel
        spread_taps = (channel >= 0) & (channel < 3) & (wanted_tap == lax.broadcasted_iota(jnp.int32, (144, 27), 1))
        tap_weights = jnp.dot(
            spread_taps.astype(F32).astype(BF16), color_ref[...], preferred_element_type=F32
        ).astype(BF16)
        crop = crops_ref[pl.ds(pl.multiple_of(block * 16, 16), 16), :]

        @pl.loop(0, pixels // tall)
        def _(m):
            at = pl.multiple_of(m * tall, tall)
            for j in range(3):
                up = jnp.dot(table_ref[j, pl.ds(at, tall), :], crop, preferred_element_type=F32)
                grid_a[pl.ds(pl.multiple_of(side + at, side), tall), j * width : (j + 1) * width] = up.astype(BF16)

        @pl.loop(0, pixels // tall)
        def _(m):
            at = pl.multiple_of(m * tall, tall)
            total = jnp.dot(patches[pl.ds(at, tall), :], tap_weights, preferred_element_type=F32)
            for i in range(3):
                total += jnp.dot(
                    grid_a[pl.ds(pl.multiple_of(at + side * i, side), tall), :],
                    first[3 * width * i : 3 * width * (i + 1), :],
                    preferred_element_type=F32,
                )
            total = jnp.maximum(total, 0.0)
            before = jnp.where(col == 0, 0.0, pltpu.roll(total, 1, 0))
            after = jnp.where(col == side - 1, 0.0, pltpu.roll(total, tall - 1, 0))
            inner = pl.ds(pl.multiple_of(side + at, side), tall)
            grid_b[inner, 0:width] = before.astype(BF16)
            grid_b[inner, width : 2 * width] = total.astype(BF16)
            grid_b[inner, 2 * width :] = after.astype(BF16)

        @pl.loop(0, pixels // tall)
        def _(m):
            at = pl.multiple_of(m * tall, tall)
            total = jnp.zeros((tall, width), F32)
            for i in range(3):
                total += jnp.dot(
                    grid_b[pl.ds(pl.multiple_of(at + side * i, side), tall), :],
                    second[3 * width * i : 3 * width * (i + 1), :],
                    preferred_element_type=F32,
                )
            total = jnp.maximum(total, 0.0).astype(BF16)
            found = lax.dot_general(
                head_ref[...], total, (((1,), (1,)), ((), ())), preferred_element_type=F32
            )
            scores[pl.ds(pl.multiple_of(block * 8, 8), head_ref.shape[0]), pl.ds(at, tall)] = found

    finished = scores[...].astype(BF16)
    step_rows = min(tiles * held, 256)
    item = lax.broadcasted_iota(jnp.int32, (step_rows, 1), 0)
    given = lax.broadcasted_iota(jnp.int32, (step_rows, 8 * CAP), 1)
    listed = lax.broadcasted_iota(jnp.int32, (step_rows, count), 1)

    @pl.loop(0, tiles * held // step_rows)
    def _(n):
        number = item + n * step_rows
        slot = jnp.max(
            jnp.where(listed == (number >> 3), jnp.broadcast_to(to_me, (step_rows, count)), -1.0), axis=1, keepdims=True
        )
        pick = ((given >> 3).astype(F32) == slot) & ((given & 7) == (number & 7))
        back_out[pl.ds(pl.multiple_of(n * step_rows, step_rows), step_rows), :] = jnp.dot(
            pick.astype(F32).astype(BF16), finished, preferred_element_type=F32
        ).astype(BF16)

    each_peer(lambda step: back_copy(step).start())
    back_in[me] = back_out[pl.ds(pl.multiple_of(me * held, held), held), :]
    each_peer(lambda step: back_copy(step).wait_recv())

    def add_back(n, total):
        return total + back_in[n].astype(F32)

    refined_ref[...] = lax.fori_loop(0, tiles, add_back, jnp.zeros(refined_ref.shape, F32)).astype(BF16)

    def drain(step):
        sum_copy(step).wait_send()
        color_copy(step).wait_send()
        crop_copy(step).wait_send()
        back_copy(step).wait_send()

    each_peer(drain)

    def drain_halo(c, carry):
        @pl.when(has_next)
        def _():
            halo_copy(0, c).wait_send()

        @pl.when(has_prev)
        def _():
            halo_copy(1, c).wait_send()

        return carry

    lax.fori_loop(0, chunks, drain_halo, 0)


def upsample_tables():
    pixels = np.arange(BLK, dtype=np.float32)
    source = np.clip((pixels + 0.5) / 8.0 - 0.5, 0.0, CELLS - 1.0)
    table = np.maximum(1.0 - np.abs(source[:, None] - np.arange(CELLS, dtype=np.float32)[None, :]), 0.0)
    tables = []
    for j in (-1, 0, 1):
        moved = np.zeros_like(table)
        for q in range(BLK):
            if 0 <= q + j < BLK:
                moved[q] = table[q + j]
        tables.append((table[:, None, :, None] * moved[None, :, None, :]).reshape(BLK * BLK, CELLS * CELLS))
    return np.stack(tables)


def pyramid(tiles, rows, cols, features, image, blocks, routes, w_one, w_rates, w_depth, w_pool, w_proj,
            w_first, w_color, w_second, w_head):
    channels, width = w_one.shape
    cells = rows * cols
    per = CAP * CELLS * CELLS
    chunks = channels // CHUNK
    edge = REACH * cols
    held = routes.shape[0] // tiles * 8
    pixels = BLK * BLK
    whole = pl.BlockSpec(memory_space=pltpu.VMEM)
    away = pl.BlockSpec(memory_space=pl.ANY)
    dma = pltpu.SemaphoreType.DMA
    image = image.transpose(0, 2, 1).reshape(-1, image.shape[1])
    first, second = w_first.reshape(9 * width, width), w_second.reshape(9 * width, width)
    return pl.pallas_call(
        functools.partial(pyramid_kernel, tiles, rows, cols, channels, width),
        out_shape=(
            jax.ShapeDtypeStruct((cells, width), BF16),
            jax.ShapeDtypeStruct((1, width), F32),
            jax.ShapeDtypeStruct((held, pixels), BF16),
        ),
        in_specs=[away, away, away, whole, away, away, away, away, away, whole, whole, whole, whole, whole],
        out_specs=(whole, whole, whole),
        scratch_shapes=[
            pltpu.VMEM(image.shape, BF16),
            pltpu.VMEM(first.shape, BF16),
            pltpu.VMEM(second.shape, BF16),
            pltpu.VMEM((per, width), BF16),
            pltpu.VMEM((16, pixels), F32),
            pltpu.VMEM((pixels + 2 * BLK, 3 * width), BF16),
            pltpu.VMEM((pixels + 2 * BLK, 3 * width), BF16),
            pltpu.VMEM((pixels, 144), BF16),
            pltpu.VMEM((CAP * 8, pixels), F32),
            pltpu.VMEM((tiles * held, pixels), BF16),
            pltpu.VMEM((tiles, held, pixels), BF16),
            pltpu.VMEM((tiles * 16, pixels), BF16),
            dma((tiles,)),
            dma((tiles,)),
            pltpu.VMEM((cells, channels), BF16),
            pltpu.VMEM(w_one.shape, BF16),
            pltpu.VMEM(w_rates.shape, BF16),
            pltpu.VMEM(w_pool.shape, BF16),
            pltpu.VMEM(w_proj.shape, BF16),
            pltpu.VMEM((2, edge, channels), BF16),
            pltpu.VMEM((cells + 2 * edge, CHUNK), F32),
            pltpu.VMEM((3, cells, CHUNK), BF16),
            pltpu.VMEM((4, cells, width), F32),
            pltpu.VMEM((1, channels), F32),
            pltpu.VMEM((tiles, 1, channels), F32),
            pltpu.VMEM((tiles, per, width), BF16),
            pltpu.VMEM((tiles, per, width), BF16),
            pltpu.VMEM((tiles, 16, pixels), BF16),
            dma((8,)),
            dma((2, chunks)),
            dma((2, chunks)),
            dma((tiles,)),
            dma((tiles,)),
            dma((tiles,)),
            dma((tiles,)),
            dma((tiles,)),
            dma((tiles,)),
        ],
        compiler_params=pltpu.CompilerParams(collective_id=0, has_side_effects=True, vmem_limit_bytes=60 << 20),
        name="pyramid",
    )(
        features.reshape(cells, channels), w_one, w_rates, w_depth.transpose(1, 0, 2), w_pool, w_proj, image, first, second,
        w_color, w_head, jnp.asarray(upsample_tables(), BF16), blocks.T, routes.T,
    )


def shards(
    tiles,
    features,
    aerial_image,
    blocks,
    routes,
    w_one,
    w_depth,
    w_rates,
    w_pool,
    w_proj,
    w_first,
    w_color,
    w_second,
    w_head,
):
    rows, cols, channels = features.shape
    width = w_one.shape[1]
    aspp, context, refined = pyramid(
        tiles, rows, cols, features, aerial_image, blocks, routes, w_one, w_rates, w_depth, w_pool, w_proj,
        w_first[0], w_color[0], w_second[0], w_head[0],
    )
    refined = refined.reshape(-1, 8, BLK * BLK)[:, : w_head.shape[1], :]
    return aspp.reshape(rows, cols, width), context.reshape(width), refined


def solution(mesh):
    return jax.shard_map(
        functools.partial(shards, mesh.shape["tile"]),
        mesh=mesh,
        in_specs=(
            P(("groups", "tile"), None, None),
            P(None, ("groups", "tile"), None),
            P("groups", None),
            P("groups", None),
            P(),
            P(),
            P(),
            P(),
            P(),
            P("tile", None, None, None),
            P("tile", None, None),
            P("tile", None, None, None),
            P("tile", None, None),
        ),
        out_specs=(
            P(("groups", "tile"), None, None),
            P("groups"),
            P(("groups", "tile"), None, None),
        ),
        check_vma=False,
    )
```

```python
import functools

import jax
import jax.numpy as jnp
import numpy as np
from jax import lax
from jax.experimental import pallas as pl
from jax.experimental.pallas import tpu as pltpu
from jax.sharding import PartitionSpec as P

BLK = 32
CAP = 4
CELLS = 4
RATES = (6, 12, 18)
REACH = 18
CHUNK = 512
F32 = jnp.float32
BF16 = jnp.bfloat16


def split_three(value):
    high = value.astype(BF16)
    rest = value - high.astype(F32)
    mid = rest.astype(BF16)
    low = (rest - mid.astype(F32)).astype(BF16)
    return high, mid, low


def exact_row_dot(row, weights):
    high, mid, low = split_three(row)
    stacked = jnp.concatenate(
        [high.astype(F32), mid.astype(F32), low.astype(F32), jnp.zeros((13, row.shape[1]), F32)], axis=0
    ).astype(BF16)
    product = jnp.dot(stacked, weights, preferred_element_type=F32)
    return product[0:1] + product[1:2] + product[2:3]


def pyramid_kernel(
    tiles, rows, cols, channels, width,
    feat_hbm, w_one_hbm, w_rates_hbm, w_depth_ref, w_pool_hbm, w_proj_hbm, image_hbm, first_hbm, second_hbm,
    color_ref, head_ref, table_ref, blocks_ref, routes_ref,
    aspp_ref, context_ref, refined_ref,
    image, first, second, crops_ref, mine_ref, grid_a, grid_b, patches, scores, back_out, back_in, colors_out, back_send, back_recv,
    feat, w_one, w_rates, w_pool, w_proj, halo, grown, depth, acc, sums, sums_in, crops_out, crops_in, colors_in,
    local_sem, halo_send, halo_recv, sum_send, sum_recv, color_send, color_recv, crop_send, crop_recv,
):
    me = lax.axis_index("tile")
    chunks = channels // CHUNK
    edge = REACH * cols
    cells = rows * cols
    count = routes_ref.shape[1]
    held = count // tiles * 8

    local = [
        pltpu.make_async_copy(source, target, local_sem.at[n])
        for n, (source, target) in enumerate(
            ((feat_hbm, feat), (w_one_hbm, w_one), (w_rates_hbm, w_rates), (w_pool_hbm, w_pool), (w_proj_hbm, w_proj),
             (image_hbm, image), (first_hbm, first), (second_hbm, second))
        )
    ]
    for copy in local:
        copy.start()

    barrier = pltpu.get_barrier_semaphore()

    def greet(step, carry):
        peer = lax.rem(me + step, tiles)
        pl.semaphore_signal(barrier, inc=1, device_id={"tile": peer}, device_id_type=pl.DeviceIdType.MESH)
        return carry

    lax.fori_loop(1, tiles, greet, 0)
    pl.semaphore_wait(barrier, tiles - 1)

    def halo_copy(side, c):
        lanes = pl.ds(pl.multiple_of(c * CHUNK, CHUNK), CHUNK)
        first = cells - edge if side == 0 else 0
        return pltpu.make_async_remote_copy(
            src_ref=feat_hbm.at[pl.ds(first, edge), lanes],
            dst_ref=halo.at[side, :, lanes],
            send_sem=halo_send.at[side, c],
            recv_sem=halo_recv.at[side, c],
            device_id={"tile": lax.rem(me + 1, tiles) if side == 0 else lax.rem(me + tiles - 1, tiles)},
            device_id_type=pl.DeviceIdType.MESH,
        )

    has_next = me < tiles - 1
    has_prev = me > 0

    def send_halo(c, carry):
        @pl.when(has_next)
        def _():
            halo_copy(0, c).start()

        @pl.when(has_prev)
        def _():
            halo_copy(1, c).start()

        return carry

    lax.fori_loop(0, chunks, send_halo, 0)

    def peer_copy(step, source, target, send, recv):
        return pltpu.make_async_remote_copy(
            src_ref=source, dst_ref=target, send_sem=send.at[step], recv_sem=recv.at[step],
            device_id={"tile": lax.rem(me + step, tiles)}, device_id_type=pl.DeviceIdType.MESH,
        )

    def sum_copy(step):
        return peer_copy(step, sums, sums_in.at[step], sum_send, sum_recv)

    def color_copy(step):
        peer = lax.rem(me + step, tiles)
        return peer_copy(step, colors_out.at[pl.ds(pl.multiple_of(peer * 16, 16), 16)], colors_in.at[me], color_send, color_recv)

    def crop_copy(step):
        peer = lax.rem(me + step, tiles)
        return peer_copy(step, crops_out.at[peer], crops_in.at[me], crop_send, crop_recv)

    def back_copy(step):
        peer = lax.rem(me + step, tiles)
        return peer_copy(
            step, back_out.at[pl.ds(pl.multiple_of(peer * held, held), held)], back_in.at[me], back_send, back_recv
        )

    def each_peer(function):
        def body(step, carry):
            function(step)
            return carry

        lax.fori_loop(1, tiles, body, 0)

    local[0].wait()

    def sum_rows(n, totals):
        block = feat[pl.ds(pl.multiple_of(n * 16, 16), 16), :].astype(F32)
        return totals + block[0:8] + block[8:16]

    totals = lax.fori_loop(0, cells // 16, sum_rows, jnp.zeros((8, channels), F32))
    sums[...] = jnp.sum(totals, axis=0, keepdims=True)
    each_peer(lambda step: sum_copy(step).start())

    local[1].wait()
    local[2].wait()
    tall = 256

    @pl.loop(0, cells // tall)
    def _(m):
        span = pl.ds(pl.multiple_of(m * tall, tall), tall)
        acc[0, span, :] = jnp.dot(feat[span, :], w_one[...], preferred_element_type=F32)
        for k in range(3):
            acc[k + 1, span, :] = jnp.zeros((tall, width), F32)

    @pl.when(jnp.logical_not(has_prev))
    def _():
        grown[0:edge, :] = jnp.zeros((edge, CHUNK), F32)

    @pl.when(jnp.logical_not(has_next))
    def _():
        grown[edge + cells :, :] = jnp.zeros((edge, CHUNK), F32)

    def widen(source, start, count, lanes):
        @pl.loop(0, count // 48)
        def _(n):
            grown[pl.ds(pl.multiple_of(start + n * 48, 8), 48), :] = source[
                pl.ds(pl.multiple_of(n * 48, 16), 48), lanes
            ].astype(F32)

    experts = routes_ref[...].astype(F32)
    square = (count, count)
    down, over = lax.broadcasted_iota(jnp.int32, square, 0), lax.broadcasted_iota(jnp.int32, square, 1)
    spread = jnp.broadcast_to(experts, square)
    upright = jnp.sum(jnp.where(down == over, spread, 0.0), axis=1, keepdims=True)
    rank = jnp.sum(jnp.where((upright == spread) & (down < over), 1.0, 0.0), axis=0, keepdims=True)
    slot_of = experts * CAP + rank
    strip_blocks = rows // CELLS
    local_row = blocks_ref[0:1, :].astype(F32) - lax.convert_element_type(me * strip_blocks, F32)
    is_mine = (local_row >= 0) & (local_row < strip_blocks)
    base = jnp.where(is_mine, local_row * (CELLS * cols) + blocks_ref[1:2, :].astype(F32) * CELLS, -1e6)
    to_me = jnp.where(experts == lax.convert_element_type(me, F32), rank, -1.0)

    def lookup(slot, values, fill):
        shape = (slot.shape[0], count)
        hit = jnp.broadcast_to(slot, shape) == jnp.broadcast_to(slot_of, shape)
        return jnp.max(jnp.where(hit, jnp.broadcast_to(values, shape), fill), axis=1, keepdims=True)

    local[5].wait()
    parts_high = image.shape[0]
    across = parts_high // 3
    group = 256
    line = lax.broadcasted_iota(jnp.int32, (group, 1), 0)
    lane = lax.broadcasted_iota(jnp.int32, (1, BLK * BLK), 1)
    source = lax.broadcasted_iota(jnp.int32, (1, parts_high), 1)
    source_channel = (source >= across).astype(jnp.int32) + (source >= 2 * across).astype(jnp.int32)
    source_block = (source - source_channel * across) // BLK
    deep = lax.broadcasted_iota(jnp.int32, (parts_high, 1), 0)
    keep = ((deep & (BLK - 1)) == (lane & (BLK - 1)))
    tall_rows = image.shape[1]
    image_row = lax.broadcasted_iota(jnp.int32, (tall_rows, 1), 0)
    colors_out[...] = jnp.zeros(colors_out.shape, BF16)

    @pl.loop(0, strip_blocks)
    def _(at):
        select = (image_row == at * BLK + (lane >> 5)).astype(F32).astype(BF16)
        strips = jnp.dot(image[...], select, preferred_element_type=F32)
        strips = jnp.where(keep, strips, 0.0).astype(BF16)

        @pl.loop(0, tiles * 16 // group)
        def _(n):
            row = line + n * group
            found = lookup((row >> 2).astype(F32), base, -1e6)
            wanted = (at * (CELLS * cols) + source_block * CELLS).astype(F32)
            chosen = ((found == wanted) & ((row & 3) == source_channel)).astype(F32).astype(BF16)
            span = pl.ds(pl.multiple_of(n * group, group), group)
            colors_out[span, :] += jnp.dot(chosen, strips, preferred_element_type=F32).astype(BF16)

    def one_chunk(c, carry):
        @pl.when(c == chunks - 2)
        def _():
            each_peer(lambda step: color_copy(step).start())

        lanes = pl.ds(pl.multiple_of(c * CHUNK, CHUNK), CHUNK)
        widen(feat, edge, cells, lanes)

        @pl.when(has_prev)
        def _():
            halo_copy(0, c).wait_recv()
            widen(halo.at[0], 0, edge, lanes)

        @pl.when(has_next)
        def _():
            halo_copy(1, c).wait_recv()
            widen(halo.at[1], edge + cells, edge, lanes)

        for half in range(CHUNK // 128):
            inner = slice(half * 128, half * 128 + 128)
            outer = pl.ds(pl.multiple_of(c * CHUNK + half * 128, 128), 128)
            for k, d in enumerate(RATES):
                taps = [
                    jnp.broadcast_to(w_depth_ref[t, k : k + 1, outer].astype(F32), (8, 128)) for t in range(9)
                ]

                def weigh(parts, column, taps=taps):
                    total = None
                    for i in range(3):
                        tap = jnp.concatenate([taps[3 * i + column]] * (parts[i].shape[0] // 8), axis=0)
                        term = parts[i] * tap
                        total = term if total is None else total + term
                    return total

                @pl.loop(0, rows // 2, unroll=4)
                def _(pair, d=d, weigh=weigh, inner=inner, k=k):
                    results = []
                    for r in range(2):
                        parts = []
                        for i in (-1, 0, 1):
                            start = pl.multiple_of((REACH + i * d + r) * cols + pair * (2 * cols), 8)
                            parts.append(grown[pl.ds(start, cols), inner])
                        low = -(-(cols - d) // 8) * 8
                        high = (d // 8) * 8
                        middle = weigh(parts, 1)
                        left = weigh([p[:low] for p in parts], 0)
                        right = weigh([p[high:] for p in parts], 2)
                        fill = jnp.zeros((d, 128), F32)
                        left = jnp.concatenate([fill, left[: cols - d]], axis=0)
                        right = jnp.concatenate([right[d - high :], fill], axis=0)
                        results.append(jnp.maximum(middle + left + right, 0.0))
                    depth[k, pl.ds(pl.multiple_of(pair * (2 * cols), 16), 2 * cols), inner] = jnp.concatenate(
                        results, axis=0
                    ).astype(BF16)

        for k in range(3):
            @pl.loop(0, cells // tall)
            def _(m, k=k):
                span = pl.ds(pl.multiple_of(m * tall, tall), tall)
                acc[k + 1, span, :] += jnp.dot(depth[k, span, :], w_rates[k, lanes, :], preferred_element_type=F32)

        return carry

    lax.fori_loop(0, chunks, one_chunk, 0)

    each_peer(lambda step: sum_copy(step).wait_recv())

    def add_sums(step, total):
        return total + sums_in[step]

    total = lax.fori_loop(1, tiles, add_sums, sums[...])
    pooled = total / (cells * tiles)
    local[3].wait()
    local[4].wait()
    context = jnp.maximum(exact_row_dot(pooled, w_pool[...]), 0.0)
    context_ref[...] = context
    offset = exact_row_dot(context, w_proj[4 * width :, :])

    @pl.loop(0, cells // tall)
    def _(m):
        span = pl.ds(pl.multiple_of(m * tall, tall), tall)
        blended = jnp.broadcast_to(offset, (tall, width))
        for k in range(4):
            branch = jnp.maximum(acc[k, span, :], 0.0).astype(BF16)
            blended += jnp.dot(branch, w_proj[k * width : (k + 1) * width, :], preferred_element_type=F32)
        aspp_ref[span, :] = jnp.maximum(blended, 0.0).astype(BF16)

    per = CAP * CELLS * CELLS
    cell_row = lax.broadcasted_iota(jnp.int32, (per, 1), 0)

    def cut(n, carry):
        slot = (n * CAP + (cell_row >> 4)).astype(F32)
        wanted = lookup(slot, base, -1e6) + (((cell_row >> 2) & 3) * cols + (cell_row & 3)).astype(F32)
        chosen = (lax.broadcasted_iota(jnp.int32, (per, cells), 1).astype(F32) == wanted).astype(F32).astype(BF16)
        crops_out[n] = jnp.dot(chosen, aspp_ref[...], preferred_element_type=F32).astype(BF16)
        return carry

    lax.fori_loop(0, tiles, cut, 0)
    crops_in[me] = crops_out[me]
    each_peer(lambda step: crop_copy(step).start())
    colors_in[me] = colors_out[pl.ds(pl.multiple_of(me * 16, 16), 16), :]
    each_peer(lambda step: color_copy(step).wait_recv())

    def add_colors(n, total):
        return total + colors_in[n].astype(F32)

    mine_ref[...] = lax.fori_loop(0, tiles, add_colors, jnp.zeros(mine_ref.shape, F32))
    side, pixels = BLK, BLK * BLK
    wide = lax.broadcasted_iota(jnp.int32, (16, pixels), 1)
    row_at, col_at = wide >> 5, wide & (side - 1)
    colors = mine_ref[...]
    pieces = []
    for i in (-1, 0, 1):
        for j in (-1, 0, 1):
            moved = colors if i == 0 and j == 0 else pltpu.roll(colors, (-(side * i + j)) % pixels, 1)
            inside = (row_at + i >= 0) & (row_at + i < side) & (col_at + j >= 0) & (col_at + j < side)
            pieces.append(jnp.where(inside, moved, 0.0))
    patches[...] = jnp.concatenate(pieces, axis=0).T.astype(BF16)
    blank = jnp.zeros((side, 3 * width), BF16)
    for grid_ref in (grid_a, grid_b):
        grid_ref[0:side, :] = blank
        grid_ref[side + pixels :, :] = blank
    tall = 512
    local[6].wait()
    local[7].wait()
    scores[...] = jnp.zeros(scores.shape, F32)
    col = lax.broadcasted_iota(jnp.int32, (tall, width), 0) & (side - 1)

    each_peer(lambda step: crop_copy(step).wait_recv())

    def add_crops(n, total):
        return total + crops_in[n].astype(F32)

    crops_ref[...] = lax.fori_loop(0, tiles, add_crops, jnp.zeros(crops_ref.shape, F32)).astype(BF16)

    @pl.loop(0, CAP)
    def _(block):
        tap_row = lax.broadcasted_iota(jnp.int32, (144, 27), 0)
        channel = (tap_row & 15) - block * 4
        wanted_tap = (tap_row >> 4) * 3 + channel
        spread_taps = (channel >= 0) & (channel < 3) & (wanted_tap == lax.broadcasted_iota(jnp.int32, (144, 27), 1))
        tap_weights = jnp.dot(
            spread_taps.astype(F32).astype(BF16), color_ref[...], preferred_element_type=F32
        ).astype(BF16)
        crop = crops_ref[pl.ds(pl.multiple_of(block * 16, 16), 16), :]

        @pl.loop(0, pixels // tall)
        def _(m):
            at = pl.multiple_of(m * tall, tall)
            for j in range(3):
                up = jnp.dot(table_ref[j, pl.ds(at, tall), :], crop, preferred_element_type=F32)
                grid_a[pl.ds(pl.multiple_of(side + at, side), tall), j * width : (j + 1) * width] = up.astype(BF16)

        @pl.loop(0, pixels // tall)
        def _(m):
            at = pl.multiple_of(m * tall, tall)
            total = jnp.dot(patches[pl.ds(at, tall), :], tap_weights, preferred_element_type=F32)
            for i in range(3):
                total += jnp.dot(
                    grid_a[pl.ds(pl.multiple_of(at + side * i, side), tall), :],
                    first[3 * width * i : 3 * width * (i + 1), :],
                    preferred_element_type=F32,
                )
            total = jnp.maximum(total, 0.0)
            before = jnp.where(col == 0, 0.0, pltpu.roll(total, 1, 0))
            after = jnp.where(col == side - 1, 0.0, pltpu.roll(total, tall - 1, 0))
            inner = pl.ds(pl.multiple_of(side + at, side), tall)
            grid_b[inner, 0:width] = before.astype(BF16)
            grid_b[inner, width : 2 * width] = total.astype(BF16)
            grid_b[inner, 2 * width :] = after.astype(BF16)

        @pl.loop(0, pixels // tall)
        def _(m):
            at = pl.multiple_of(m * tall, tall)
            total = jnp.zeros((tall, width), F32)
            for i in range(3):
                total += jnp.dot(
                    grid_b[pl.ds(pl.multiple_of(at + side * i, side), tall), :],
                    second[3 * width * i : 3 * width * (i + 1), :],
                    preferred_element_type=F32,
                )
            total = jnp.maximum(total, 0.0).astype(BF16)
            found = lax.dot_general(
                head_ref[...], total, (((1,), (1,)), ((), ())), preferred_element_type=F32
            )
            scores[pl.ds(pl.multiple_of(block * 8, 8), head_ref.shape[0]), pl.ds(at, tall)] = found

    finished = scores[...].astype(BF16)
    step_rows = min(tiles * held, 256)
    item = lax.broadcasted_iota(jnp.int32, (step_rows, 1), 0)
    given = lax.broadcasted_iota(jnp.int32, (step_rows, 8 * CAP), 1)
    listed = lax.broadcasted_iota(jnp.int32, (step_rows, count), 1)

    @pl.loop(0, tiles * held // step_rows)
    def _(n):
        number = item + n * step_rows
        slot = jnp.max(
            jnp.where(listed == (number >> 3), jnp.broadcast_to(to_me, (step_rows, count)), -1.0), axis=1, keepdims=True
        )
        pick = ((given >> 3).astype(F32) == slot) & ((given & 7) == (number & 7))
        back_out[pl.ds(pl.multiple_of(n * step_rows, step_rows), step_rows), :] = jnp.dot(
            pick.astype(F32).astype(BF16), finished, preferred_element_type=F32
        ).astype(BF16)

    each_peer(lambda step: back_copy(step).start())
    back_in[me] = back_out[pl.ds(pl.multiple_of(me * held, held), held), :]
    each_peer(lambda step: back_copy(step).wait_recv())

    def add_back(n, total):
        return total + back_in[n].astype(F32)

    refined_ref[...] = lax.fori_loop(0, tiles, add_back, jnp.zeros(refined_ref.shape, F32)).astype(BF16)

    def drain(step):
        sum_copy(step).wait_send()
        color_copy(step).wait_send()
        crop_copy(step).wait_send()
        back_copy(step).wait_send()

    each_peer(drain)

    def drain_halo(c, carry):
        @pl.when(has_next)
        def _():
            halo_copy(0, c).wait_send()

        @pl.when(has_prev)
        def _():
            halo_copy(1, c).wait_send()

        return carry

    lax.fori_loop(0, chunks, drain_halo, 0)


def upsample_tables():
    pixels = np.arange(BLK, dtype=np.float32)
    source = np.clip((pixels + 0.5) / 8.0 - 0.5, 0.0, CELLS - 1.0)
    table = np.maximum(1.0 - np.abs(source[:, None] - np.arange(CELLS, dtype=np.float32)[None, :]), 0.0)
    tables = []
    for j in (-1, 0, 1):
        moved = np.zeros_like(table)
        for q in range(BLK):
            if 0 <= q + j < BLK:
                moved[q] = table[q + j]
        tables.append((table[:, None, :, None] * moved[None, :, None, :]).reshape(BLK * BLK, CELLS * CELLS))
    return np.stack(tables)


def pyramid(tiles, rows, cols, features, image, blocks, routes, w_one, w_rates, w_depth, w_pool, w_proj,
            w_first, w_color, w_second, w_head):
    channels, width = w_one.shape
    cells = rows * cols
    per = CAP * CELLS * CELLS
    chunks = channels // CHUNK
    edge = REACH * cols
    held = routes.shape[0] // tiles * 8
    pixels = BLK * BLK
    whole = pl.BlockSpec(memory_space=pltpu.VMEM)
    away = pl.BlockSpec(memory_space=pl.ANY)
    dma = pltpu.SemaphoreType.DMA
    image = image.transpose(0, 2, 1).reshape(-1, image.shape[1])
    first, second = w_first.reshape(9 * width, width), w_second.reshape(9 * width, width)
    return pl.pallas_call(
        functools.partial(pyramid_kernel, tiles, rows, cols, channels, width),
        out_shape=(
            jax.ShapeDtypeStruct((cells, width), BF16),
            jax.ShapeDtypeStruct((1, width), F32),
            jax.ShapeDtypeStruct((held, pixels), BF16),
        ),
        in_specs=[away, away, away, whole, away, away, away, away, away, whole, whole, whole, whole, whole],
        out_specs=(whole, whole, whole),
        scratch_shapes=[
            pltpu.VMEM(image.shape, BF16),
            pltpu.VMEM(first.shape, BF16),
            pltpu.VMEM(second.shape, BF16),
            pltpu.VMEM((per, width), BF16),
            pltpu.VMEM((16, pixels), F32),
            pltpu.VMEM((pixels + 2 * BLK, 3 * width), BF16),
            pltpu.VMEM((pixels + 2 * BLK, 3 * width), BF16),
            pltpu.VMEM((pixels, 144), BF16),
            pltpu.VMEM((CAP * 8, pixels), F32),
            pltpu.VMEM((tiles * held, pixels), BF16),
            pltpu.VMEM((tiles, held, pixels), BF16),
            pltpu.VMEM((tiles * 16, pixels), BF16),
            dma((tiles,)),
            dma((tiles,)),
            pltpu.VMEM((cells, channels), BF16),
            pltpu.VMEM(w_one.shape, BF16),
            pltpu.VMEM(w_rates.shape, BF16),
            pltpu.VMEM(w_pool.shape, BF16),
            pltpu.VMEM(w_proj.shape, BF16),
            pltpu.VMEM((2, edge, channels), BF16),
            pltpu.VMEM((cells + 2 * edge, CHUNK), F32),
            pltpu.VMEM((3, cells, CHUNK), BF16),
            pltpu.VMEM((4, cells, width), F32),
            pltpu.VMEM((1, channels), F32),
            pltpu.VMEM((tiles, 1, channels), F32),
            pltpu.VMEM((tiles, per, width), BF16),
            pltpu.VMEM((tiles, per, width), BF16),
            pltpu.VMEM((tiles, 16, pixels), BF16),
            dma((8,)),
            dma((2, chunks)),
            dma((2, chunks)),
            dma((tiles,)),
            dma((tiles,)),
            dma((tiles,)),
            dma((tiles,)),
            dma((tiles,)),
            dma((tiles,)),
        ],
        compiler_params=pltpu.CompilerParams(collective_id=0, has_side_effects=True, vmem_limit_bytes=60 << 20),
        name="pyramid",
    )(
        features.reshape(cells, channels), w_one, w_rates, w_depth.transpose(1, 0, 2), w_pool, w_proj, image, first, second,
        w_color, w_head, jnp.asarray(upsample_tables(), BF16), blocks.T, routes.T,
    )


def shards(
    tiles,
    features,
    aerial_image,
    blocks,
    routes,
    w_one,
    w_depth,
    w_rates,
    w_pool,
    w_proj,
    w_first,
    w_color,
    w_second,
    w_head,
):
    rows, cols, channels = features.shape
    width = w_one.shape[1]
    aspp, context, refined = pyramid(
        tiles, rows, cols, features, aerial_image, blocks, routes, w_one, w_rates, w_depth, w_pool, w_proj,
        w_first[0], w_color[0], w_second[0], w_head[0],
    )
    refined = refined.reshape(-1, 8, BLK * BLK)[:, : w_head.shape[1], :]
    return aspp.reshape(rows, cols, width), context.reshape(width), refined


def solution(mesh):
    return jax.shard_map(
        functools.partial(shards, mesh.shape["tile"]),
        mesh=mesh,
        in_specs=(
            P(("groups", "tile"), None, None),
            P(None, ("groups", "tile"), None),
            P("groups", None),
            P("groups", None),
            P(),
            P(),
            P(),
            P(),
            P(),
            P("tile", None, None, None),
            P("tile", None, None),
            P("tile", None, None, None),
            P("tile", None, None),
        ),
        out_specs=(
            P(("groups", "tile"), None, None),
            P("groups"),
            P(("groups", "tile"), None, None),
        ),
        check_vma=False,
    )
```
